32 devices in a mesh: groups: 2 (over y), tile: 4 (over z), pass: 2 (over x), row: 2 (over core).
Axes of the slice: x: 2, y: 2, z: 4, core: 2. Of those that a mesh axis runs over, the one named last changes fastest.
Arguments:
- revisits: bfloat16 [32, 8, 64, 1024], P(('groups', 'pass'), ('tile', 'row')), parts along dimension 0, may hold values from -6 to 6
- shifts: int32 [32, 2], P(('groups', 'pass')), parts along dimension 0, may hold values from -32 to 32, as said below
- flags: int32 [32, 8], P('groups', ('tile', 'row')), parts along dimension 0, may hold values from 0 to 1, as said below
- norm1_gain: float32 [64], replicated, may hold values from 0.1 to 1.9
- w_query: bfloat16 [64, 64], replicated, may hold values from -0.75 to 0.75
- w_key: bfloat16 [64, 64], replicated, may hold values from -0.75 to 0.75
- w_value: bfloat16 [64, 64], replicated, may hold values from -0.75 to 0.75
- query_gain: float32 [64], replicated, may hold values from 0.1 to 1.9
- key_gain: float32 [64], replicated, may hold values from 0.1 to 1.9
- w_out: bfloat16 [64, 64], replicated, may hold values from -0.75 to 0.75
- norm2_gain: float32 [64], replicated, may hold values from 0.1 to 1.9
- w_in: bfloat16 [64, 128], replicated, may hold values from -0.75 to 0.75
- w_back: bfloat16 [128, 64], replicated, may hold values from -0.5 to 0.5
- conv_first: bfloat16 [3, 3, 64, 64], replicated, may hold values from -0.75 to 0.75
- conv_second: bfloat16 [3, 3, 64, 9], replicated, may hold values from -0.25 to 0.25
Outputs:
- output: float32 [16, 9, 1024], P(('groups', 'pass'), None, ('tile', 'row')), parts along dimension 0
The draws below stay inside these ranges and needn't reach their ends.
There are 2 independent parts, one for each index of `groups`. The reference program is written for one: setup_inputs(seed, part) draws one part's arguments, and reference() takes and returns one part's arrays. A program takes and returns all parts, laid end to end along the dimension named above; an argument that names none is the same for every part. Nothing has to cross between parts.
Inputs may be any that keep to these rules, and one draw needn't show every extreme that they name: `shifts`: some revisit has row shift 32, some -32, some column shift 32 and some -32. `flags`: every row band has at least one cloud-free revisit.
All inputs are finite; a program needn't handle non-finite values.
Results may differ from the reference program's by a relative error of at most 0.007.
Values may be sent and summed in bfloat16 or wider, within the bound.
A program may use at most 128 MiB of HBM per device.

```python
import math
import jax
import jax.numpy as jnp
from jax import lax

R = 16
C = 64
HEADS = 4
MLP = 128
OUT = 9
BR = 128
NBANDS = 8
NCOLS = 8
NROWS = 1024


def draw_shifts(key, part):
    first, second = jax.random.split(jax.random.fold_in(key, 11))
    values = jax.random.randint(first, (R, 2), -32, 33)
    picks = jax.random.permutation(second, R)
    values = values.at[picks[0], 0].set(32)
    values = values.at[picks[1], 0].set(-32)
    values = values.at[picks[2], 1].set(32)
    values = values.at[picks[3], 1].set(-32)
    return values.astype(jnp.int32)


def draw_flags(key, part):
    first, second = jax.random.split(jax.random.fold_in(key, 23))
    coins = jax.random.randint(first, (R, NBANDS), 0, 10) < 7
    keeper = jax.random.randint(second, (NBANDS,), 0, R)
    forced = jnp.arange(R)[:, None] == keeper[None, :]
    return (coins | forced).astype(jnp.int32)


def block_levels(key, shape, cuts, smallest, top_value):
    level, own = 1.0, jax.random.fold_in(key, 6)
    for dim, blocks in cuts:
        steps = jnp.exp(jax.random.uniform(jax.random.fold_in(own, dim), (blocks,), jnp.float32, smallest / len(cuts), top_value / len(cuts)))
        level = level * jnp.repeat(steps, shape[dim] // blocks).reshape([-1 if axis == dim else 1 for axis in range(len(shape))])
    return level


def bell_draw(rng, dims, spread, most, shards=(), held_as=jnp.bfloat16):
    level = block_levels(rng, dims, shards, -0.22, 0.18) if shards else 1.0
    array = jax.random.normal(rng, dims, jnp.float32) * spread * level
    return jnp.minimum(jnp.maximum(array, -most), most).astype(held_as)


def setup_inputs(seed: int = 0, part: int = 0) -> dict:
    seeds = jax.random.split(jax.random.key(seed), 16)
    own_keys = jax.random.split(jax.random.fold_in(seeds[15], part), 16)
    return {
        "revisits": bell_draw(own_keys[0], (R, NCOLS, C, NROWS), 1.0, 6.0, ((0, 2), (1, 8))),
        "shifts": draw_shifts(jax.random.fold_in(jax.random.fold_in(seeds[15], part), 71), part),
        "flags": draw_flags(jax.random.fold_in(jax.random.fold_in(seeds[15], part), 71), part),
        "norm1_gain": jnp.clip(1.0 + 0.18 * jax.random.normal(seeds[3], (C,), jnp.float32), 0.1, 1.9),
        "w_query": bell_draw(seeds[4], (C, C), C ** -0.5, 0.75),
        "w_key": bell_draw(seeds[5], (C, C), C ** -0.5, 0.75),
        "w_value": bell_draw(seeds[6], (C, C), C ** -0.5, 0.75),
        "query_gain": jnp.clip(1.0 + 0.18 * jax.random.normal(seeds[7], (C,), jnp.float32), 0.1, 1.9),
        "key_gain": jnp.clip(1.0 + 0.18 * jax.random.normal(seeds[8], (C,), jnp.float32), 0.1, 1.9),
        "w_out": bell_draw(seeds[9], (C, C), C ** -0.5, 0.75),
        "norm2_gain": jnp.clip(1.0 + 0.18 * jax.random.normal(seeds[10], (C,), jnp.float32), 0.1, 1.9),
        "w_in": bell_draw(seeds[11], (C, MLP), C ** -0.5, 0.75),
        "w_back": bell_draw(seeds[12], (MLP, C), MLP ** -0.5, 0.5),
        "conv_first": bell_draw(seeds[13], (3, 3, C, C), C ** -0.5, 0.75),
        "conv_second": bell_draw(seeds[14], (3, 3, C, OUT), (9 * C) ** -0.5, 0.25),
    }


eps = 1e-05
reach = 32

def rounded(values):
    return lax.optimization_barrier(values.astype(jnp.bfloat16)).astype(jnp.float32)

def rms_scale(values, gain):
    mean = lax.optimization_barrier(jnp.mean(values * values, axis=-2, keepdims=True))
    return values * lax.rsqrt(mean + eps) * gain[:, None]

def join_cells(cells_in, mask, norm1_gain, w_query, w_key, w_value, query_gain, key_gain, w_out, norm2_gain, w_in, w_back):
    f32 = jnp.float32
    count, width, chans, rows = cells_in.shape
    cells = cells_in.astype(f32)
    normed = rounded(rms_scale(cells, norm1_gain))
    query = jnp.einsum('rjcy,cd->rjdy', normed, w_query.astype(f32))
    keys = jnp.einsum('rjcy,cd->rjdy', normed, w_key.astype(f32))
    values = rounded(jnp.einsum('rjcy,cd->rjdy', normed, w_value.astype(f32)))
    q_hat = rounded(rms_scale(query, query_gain))
    k_hat = rounded(rms_scale(keys, key_gain))
    head_size = chans // HEADS
    q_heads = q_hat.reshape(count, width, HEADS, head_size, rows)
    k_heads = k_hat.reshape(count, width, HEADS, head_size, rows)
    v_heads = values.reshape(count, width, HEADS, head_size, rows)
    scores = jnp.einsum('rjhey,sjhey->hrsjy', q_heads, k_heads) * (1.0 / math.sqrt(head_size))
    weights = jnp.exp(scores) * mask[None, None, :, None, None]
    probs = rounded(weights / lax.optimization_barrier(jnp.sum(weights, axis=2, keepdims=True)))
    mixed = rounded(jnp.einsum('hrsjy,sjhey->rjhey', probs, v_heads)).reshape(count, width, chans, rows)
    hidden = cells + jnp.einsum('rjcy,cd->rjdy', mixed, w_out.astype(f32))
    normed_two = rounded(rms_scale(hidden, norm2_gain))
    inner = rounded(jax.nn.gelu(jnp.einsum('rjcy,cm->rjmy', normed_two, w_in.astype(f32)), approximate=True))
    tokens = hidden + jnp.einsum('rjmy,mc->rjcy', inner, w_back.astype(f32))
    total = lax.optimization_barrier(jnp.sum(tokens * mask[:, None, None, None], axis=0))
    return (total / jnp.sum(mask)).astype(jnp.bfloat16)

def convolve(values, weights):
    cols = values.shape[0]
    rows = values.shape[2]
    wide = jnp.pad(values.astype(jnp.float32), ((1, 1), (0, 0), (1, 1)))
    total = jnp.zeros((cols, weights.shape[3], rows), jnp.float32)
    for across in range(3):
        for down in range(3):
            total = total + jnp.einsum('xcy,co->xoy', wide[across:across + cols, :, down:down + rows], weights[across, down].astype(jnp.float32))
    return total

def reference(revisits, shifts, flags, norm1_gain, w_query, w_key, w_value, query_gain, key_gain, w_out, norm2_gain, w_in, w_back, conv_first, conv_second):
    padded = jnp.pad(revisits, ((0, 0), (reach, reach), (0, 0), (reach, reach)))

    def band_join(index):
        slab = lax.dynamic_slice_in_dim(padded, index * BR, BR + 2 * reach, 3)

        def single(entry, offset):
            return lax.dynamic_slice(entry, (reach + offset[1], jnp.int32(0), reach + offset[0]), (NCOLS, C, BR))
        aligned = jax.vmap(single)(slab, shifts)
        mask = lax.dynamic_slice_in_dim(flags, index, 1, 1)[:, 0].astype(jnp.float32)
        return join_cells(aligned, mask, norm1_gain, w_query, w_key, w_value, query_gain, key_gain, w_out, norm2_gain, w_in, w_back)
    bands = lax.map(band_join, jnp.arange(NBANDS, dtype=jnp.int32))
    joined = jnp.transpose(bands, (1, 2, 0, 3)).reshape(NCOLS, C, NROWS)
    act = jax.nn.gelu(convolve(joined, conv_first), approximate=True).astype(jnp.bfloat16)
    return convolve(act, conv_second)
```

```python
import functools
import math

import jax
import jax.numpy as jnp
import numpy as np
from jax import lax
from jax.experimental import pallas as pl
from jax.experimental.pallas import tpu as pltpu
from jax.sharding import PartitionSpec as P

HEADS = 4
eps = 1e-05
f32 = jnp.float32
half = jnp.bfloat16
MESH = pl.DeviceIdType.MESH
GRANT = 60 * 1024 * 1024


def whole(space=pltpu.VMEM):
    return pl.BlockSpec(memory_space=space)


def dot_t(weights, values):
    return lax.dot_general(
        weights, values, (((0,), (0,)), ((), ())), preferred_element_type=f32
    )


def shift_kernel(shifts, x_ref, o_ref, meta_ref):
    bands, per, count, chans, rows = o_ref.shape
    lane = lax.broadcasted_iota(jnp.int32, (chans, rows), 1)

    def one(r, carry):
        offset = shifts[r, 0]
        amount = lax.rem(2 * rows - offset, rows)
        pos = lane + offset
        for c in range(per):
            rolled = [
                pltpu.roll(x_ref[r, c, :, t * rows : (t + 1) * rows].astype(f32), amount, 1)
                for t in range(bands)
            ]
            zero = jnp.zeros((chans, rows), f32)
            for t in range(bands):
                low = rolled[t - 1] if t else zero
                high = rolled[t + 1] if t + 1 < bands else zero
                out = jnp.where(pos < 0, low, jnp.where(pos >= rows, high, rolled[t]))
                o_ref[t, c, r] = out.astype(half)
        meta_ref[pl.ds(r, 1), :] = jnp.full((1, meta_ref.shape[1]), shifts[r, 1], jnp.int32)
        return carry

    lax.fori_loop(0, count, one, 0)


def gather_kernel(sizes, s_ref, m_ref, o_ref, mo_ref, loc, send1, recv1, send2, recv2, sendm, recvm):
    nrow, bands, passes = sizes
    p = lax.axis_index("pass")
    b = lax.axis_index("tile") * nrow + lax.axis_index("row")

    def band_id(k):
        return {"tile": k // nrow, "row": k % nrow}

    barrier = pltpu.get_barrier_semaphore()
    for k in range(1, bands):
        pl.semaphore_signal(
            barrier, inc=1, device_id=band_id((b + k) % bands), device_id_type=MESH
        )
    for k in range(1, passes):
        pl.semaphore_signal(
            barrier, inc=1, device_id={"pass": (p + k) % passes}, device_id_type=MESH
        )
    pl.semaphore_wait(barrier, bands + passes - 2)

    own = pltpu.make_async_copy(s_ref.at[b], o_ref.at[p, b], loc.at[0])
    own.start()
    own_meta = pltpu.make_async_copy(m_ref, mo_ref.at[p], loc.at[1])
    own_meta.start()
    pending = []

    def forward(src, slot, index):
        for k in range(1, passes):
            copy = pltpu.make_async_remote_copy(
                src_ref=src,
                dst_ref=o_ref.at[p, index],
                send_sem=send2.at[k - 1, slot],
                recv_sem=recv2.at[k - 1, slot],
                device_id={"pass": (p + k) % passes},
                device_id_type=MESH,
            )
            copy.start()
            pending.append(copy)

    for k in range(1, passes):
        copy = pltpu.make_async_remote_copy(
            src_ref=m_ref,
            dst_ref=mo_ref.at[p],
            send_sem=sendm.at[k - 1],
            recv_sem=recvm.at[k - 1],
            device_id={"pass": (p + k) % passes},
            device_id_type=MESH,
        )
        copy.start()
        pending.append(copy)
    forward(s_ref.at[b], 0, b)
    first = []
    order = [k for k in range(1, bands)]
    order.sort(key=lambda k: min(k, bands - k))
    for k in reversed(order):
        peer = (b + k) % bands
        copy = pltpu.make_async_remote_copy(
            src_ref=s_ref.at[peer],
            dst_ref=o_ref.at[p, b],
            send_sem=send1.at[k - 1],
            recv_sem=recv1.at[k - 1],
            device_id=band_id(peer),
            device_id_type=MESH,
        )
        copy.start()
        first.append((k, copy))
    for k, copy in first:
        copy.wait_recv()
        source = (b + bands - k) % bands
        forward(o_ref.at[p, source], k, source)
    for _, copy in first:
        copy.wait_send()
    for copy in pending:
        copy.wait()
    own.wait()
    own_meta.wait()


def rms(values, gain):
    mean = jnp.mean(values * values, axis=0, keepdims=True)
    return values * lax.rsqrt(mean + eps) * gain


def join_kernel(
    cols,
    meta,
    flags,
    x_ref,
    gains,
    spread,
    gather,
    w_query,
    w_key,
    w_value,
    w_out,
    w_in,
    w_back,
    o_ref,
    cells,
    q_s,
    k_s,
    v_s,
    mask_s,
    total_s,
):
    passes, ncols, per, chans, rows = x_ref.shape
    count = passes * per
    base = lax.axis_index("pass") * cols
    g1, gq, gk, g2 = (jnp.concatenate([gains[i], gains[i]], axis=1) for i in range(4))
    group = lax.broadcasted_iota(jnp.int32, mask_s.shape, 0) % count
    mask = jnp.zeros(mask_s.shape, f32)
    flag_sum = f32(0)
    for s in range(count):
        flag = flags[s, 0].astype(f32)
        flag_sum = flag_sum + flag
        mask = jnp.where(group == s, flag, mask)
    mask_s[...] = mask

    def column(x, carry):
        def project(j, carry):
            pair = []
            for i in range(2):
                r = 2 * j + i
                pr, rr = r // per, r % per
                col = base + x + meta[pr, rr, 0]
                inside = (col >= 0) & (col < ncols)
                value = x_ref[pr, jnp.clip(col, 0, ncols - 1), rr].astype(f32)
                pair.append(jnp.where(inside, value, 0.0))
            both = jnp.concatenate(pair, axis=1)
            cells[j] = both
            normed = rms(both, g1).astype(half)
            q_s[j] = rms(dot_t(w_query[...], normed), gq).astype(half)
            k_hat = rms(dot_t(w_key[...], normed), gk).astype(half)
            value = dot_t(w_value[...], normed).astype(half).astype(f32)
            for i in range(2):
                k_s[2 * j + i] = k_hat[:, i * rows : (i + 1) * rows]
                v_s[2 * j + i] = value[:, i * rows : (i + 1) * rows]
            return carry

        lax.fori_loop(0, count // 2, project, 0)
        total_s[...] = jnp.zeros_like(total_s)

        def attend(j, carry):
            keys = k_s[...]
            q_pair = q_s[j]
            prods = [
                (keys * q_pair[:, i * rows : (i + 1) * rows][None]).reshape(count * chans, rows)
                for i in range(2)
            ]
            scores = jnp.dot(
                spread[...], jnp.concatenate(prods, axis=1), preferred_element_type=f32
            )
            weights = jnp.exp(scores) * mask_s[...]
            weights = weights.reshape(HEADS, count, 2 * rows)
            probs = weights / jnp.sum(weights, axis=1, keepdims=True)
            probs = probs.reshape(HEADS * count, 2 * rows).astype(half)
            mixed = jnp.zeros((chans, 2 * rows), f32)
            for s in range(count):
                wide = jnp.dot(gather[s], probs, preferred_element_type=f32)
                value = v_s[s]
                mixed = mixed + wide * jnp.concatenate([value, value], axis=1)
            hidden = cells[j] + dot_t(w_out[...], mixed.astype(half))
            normed = rms(hidden, g2).astype(half)
            inner = jax.nn.gelu(dot_t(w_in[...], normed), approximate=True).astype(half)
            tokens = hidden + dot_t(w_back[...], inner)
            for i in range(2):
                flag = flags[2 * j + i, 0].astype(f32)
                total_s[...] += tokens[:, i * rows : (i + 1) * rows] * flag
            return carry

        lax.fori_loop(0, count // 2, attend, 0)
        o_ref[x] = (total_s[...] / flag_sum).astype(half)
        return carry

    lax.fori_loop(0, cols, column, 0)


MOVES = [(dp, db) for dp in (-1, 0, 1) for db in (-1, 0, 1) if (dp, db) != (0, 0)]


def decode_kernel(sizes, j_ref, w1, w2, o_ref, *scratch):
    nrow, bands, passes = sizes
    bufs = scratch[: len(MOVES)]
    taps, acts, send, recv = scratch[len(MOVES) :]
    cols, chans, rows = j_ref.shape
    p = lax.axis_index("pass")
    b = lax.axis_index("tile") * nrow + lax.axis_index("row")

    def exists(dp, db):
        ok = jnp.bool_(True)
        if dp:
            ok = ok & (p + dp >= 0) & (p + dp < passes)
        if db:
            ok = ok & (b + db >= 0) & (b + db < bands)
        return ok

    def target(dp, db):
        k = b + db
        return {"pass": p + dp, "tile": k // nrow, "row": k % nrow}

    barrier = pltpu.get_barrier_semaphore()
    neighbours = jnp.int32(0)
    for dp, db in MOVES:
        there = exists(dp, db)
        neighbours = neighbours + there.astype(jnp.int32)

        @pl.when(there)
        def _():
            pl.semaphore_signal(barrier, inc=1, device_id=target(dp, db), device_id_type=MESH)

    pl.semaphore_wait(barrier, neighbours)

    def copy_of(n):
        dp, db = MOVES[n]
        src = j_ref
        if dp:
            src = j_ref.at[pl.ds(cols - 2 if dp > 0 else 0, 2)]
        return pltpu.make_async_remote_copy(
            src_ref=src,
            dst_ref=bufs[n],
            send_sem=send.at[n],
            recv_sem=recv.at[n],
            device_id=target(dp, db),
            device_id_type=MESH,
        )

    for n, (dp, db) in enumerate(MOVES):

        @pl.when(exists(dp, db))
        def _():
            copy_of(n).start()

    for n, (dp, db) in enumerate(MOVES):

        @pl.when(exists(-dp, -db))
        def _():
            copy_of(n).wait_recv()

        @pl.when(jnp.logical_not(exists(-dp, -db)))
        def _():
            bufs[n][...] = jnp.zeros_like(bufs[n])

    def side(dp, db):
        return bufs[MOVES.index((-dp, -db))]

    lane = lax.broadcasted_iota(jnp.int32, (chans, rows), 1)
    wide_lane = lax.broadcasted_iota(jnp.int32, (chans, 2 * rows), 1)

    def widen(values):
        last = 2 * rows - 1
        return jnp.concatenate(
            [
                pltpu.roll(values, 1, 1).astype(half),
                values.astype(half),
                pltpu.roll(values, last, 1).astype(half),
            ],
            axis=0,
        )

    for n in range(cols + 4):
        dp = -1 if n < 2 else (1 if n >= cols + 2 else 0)
        at = n if dp < 0 else (n - cols - 2 if dp > 0 else n - 2)
        middle = j_ref[at] if dp == 0 else side(dp, 0)[at]
        border = jnp.where(
            lane < rows // 2, side(dp, 1)[at].astype(f32), side(dp, -1)[at].astype(f32)
        )
        taps[n] = widen(jnp.concatenate([middle.astype(f32), border], axis=1))
    row_pos = b * rows + jnp.where(wide_lane < rows + rows // 2, wide_lane, wide_lane - 2 * rows)
    row_inside = (row_pos >= 0) & (row_pos < bands * rows)
    for n in range(cols + 2):
        near = taps[n : n + 3].reshape(9 * chans, 2 * rows)
        act = jax.nn.gelu(dot_t(w1[...], near), approximate=True)
        col_pos = p * cols + n - 1
        inside = row_inside & (col_pos >= 0) & (col_pos < passes * cols)
        acts[n] = widen(jnp.where(inside, act, 0.0))
    for n in range(cols):
        near = acts[n : n + 3, :, :rows].reshape(9 * chans, rows)
        o_ref[n] = dot_t(w2[...], near)

    for n, (dp, db) in enumerate(MOVES):

        @pl.when(exists(dp, db))
        def _():
            copy_of(n).wait_send()


def local(
    nrow,
    bands,
    passes,
    revisits,
    shifts,
    flags,
    norm1_gain,
    w_query,
    w_key,
    w_value,
    query_gain,
    key_gain,
    w_out,
    norm2_gain,
    w_in,
    w_back,
    conv_first,
    conv_second,
):
    sizes = (nrow, bands, passes)
    per, own_cols, chans, all_rows = revisits.shape
    rows = all_rows // bands
    ncols = own_cols * bands
    cols = ncols // passes
    count = per * passes
    side_effects = dict(has_side_effects=True, vmem_limit_bytes=GRANT)
    shifted, meta = pl.pallas_call(
        shift_kernel,
        out_shape=(
            jax.ShapeDtypeStruct((bands, own_cols, per, chans, rows), half),
            jax.ShapeDtypeStruct((per, 128), jnp.int32),
        ),
        in_specs=[whole(pltpu.SMEM), whole()],
        out_specs=(whole(), whole()),
        compiler_params=pltpu.CompilerParams(vmem_limit_bytes=GRANT),
        name="row_shift",
    )(shifts, revisits)
    dma = pltpu.SemaphoreType.DMA
    others = max(passes - 1, 1)
    banded, metas = pl.pallas_call(
        functools.partial(gather_kernel, sizes),
        out_shape=(
            jax.ShapeDtypeStruct((passes, bands, own_cols, per, chans, rows), half),
            jax.ShapeDtypeStruct((passes, per, 128), jnp.int32),
        ),
        in_specs=[whole(), whole()],
        out_specs=(whole(), whole()),
        scratch_shapes=[
            dma((2,)),
            dma((bands,)),
            dma((bands,)),
            dma((others, bands)),
            dma((others, bands)),
            dma((others,)),
            dma((others,)),
        ],
        compiler_params=pltpu.CompilerParams(collective_id=0, **side_effects),
        name="exchange",
    )(shifted, meta)
    banded = banded.reshape(passes, ncols, per, chans, rows)
    gains = jnp.broadcast_to(
        jnp.stack([norm1_gain, query_gain, key_gain, norm2_gain])[:, :, None], (4, chans, rows)
    )
    head_size = chans // HEADS
    heads = np.arange(HEADS * count) // count
    seen = np.arange(HEADS * count) % count
    at = np.arange(count * chans)
    match = (seen[:, None] == at[None] // chans) & (heads[:, None] == at[None] % chans // head_size)
    spread = jnp.asarray(match * (1.0 / math.sqrt(head_size)), half)
    gather = jnp.asarray(match.T.reshape(count, chans, HEADS * count), half)
    joined = pl.pallas_call(
        functools.partial(join_kernel, cols),
        out_shape=jax.ShapeDtypeStruct((cols, chans, rows), half),
        in_specs=[whole(pltpu.SMEM), whole(pltpu.SMEM)] + [whole()] * 10,
        out_specs=whole(),
        scratch_shapes=[
            pltpu.VMEM((count // 2, chans, 2 * rows), f32),
            pltpu.VMEM((count // 2, chans, 2 * rows), half),
            pltpu.VMEM((count, chans, rows), half),
            pltpu.VMEM((count, chans, rows), f32),
            pltpu.VMEM((HEADS * count, 2 * rows), f32),
            pltpu.VMEM((chans, rows), f32),
        ],
        compiler_params=pltpu.CompilerParams(vmem_limit_bytes=GRANT),
        name="join",
    )(metas, flags, banded, gains, spread, gather, w_query, w_key, w_value, w_out, w_in, w_back)
    outs = conv_second.shape[3]
    return pl.pallas_call(
        functools.partial(decode_kernel, sizes),
        out_shape=jax.ShapeDtypeStruct((cols, outs, rows), f32),
        in_specs=[whole()] * 3,
        out_specs=whole(),
        scratch_shapes=[
            pltpu.VMEM((2 if dp else cols, chans, rows), half) for dp, db in MOVES
        ]
        + [
            pltpu.VMEM((cols + 4, 3 * chans, 2 * rows), half),
            pltpu.VMEM((cols + 2, 3 * chans, 2 * rows), half),
            dma((len(MOVES),)),
            dma((len(MOVES),)),
        ],
        compiler_params=pltpu.CompilerParams(collective_id=1, **side_effects),
        name="decode",
    )(joined, conv_first.reshape(9 * chans, -1), conv_second.reshape(9 * chans, outs))


def solution(mesh):
    shape = mesh.shape
    fixed = [P()] * 12
    return jax.shard_map(
        functools.partial(local, shape["row"], shape["tile"] * shape["row"], shape["pass"]),
        mesh=mesh,
        in_specs=(
            P(("groups", "pass"), ("tile", "row"), None, None),
            P(("groups", "pass"), None),
            P("groups", ("tile", "row")),
            *fixed,
        ),
        out_specs=P(("groups", "pass"), None, ("tile", "row")),
        check_vma=False,
    )
```

```python
import functools
import math

import jax
import jax.numpy as jnp
import numpy as np
from jax import lax
from jax.experimental import pallas as pl
from jax.experimental.pallas import tpu as pltpu
from jax.sharding import PartitionSpec as P

HEADS = 4
eps = 1e-05
f32 = jnp.float32
half = jnp.bfloat16
MESH = pl.DeviceIdType.MESH
GRANT = 60 * 1024 * 1024


def whole(space=pltpu.VMEM):
    return pl.BlockSpec(memory_space=space)


def dot_t(weights, values):
    return lax.dot_general(
        weights, values, (((0,), (0,)), ((), ())), preferred_element_type=f32
    )


def shift_kernel(shifts, x_ref, o_ref, meta_ref):
    bands, per, count, chans, rows = o_ref.shape
    lane = lax.broadcasted_iota(jnp.int32, (chans, rows), 1)

    def one(r, carry):
        offset = shifts[r, 0]
        amount = lax.rem(2 * rows - offset, rows)
        pos = lane + offset
        for c in range(per):
            rolled = [
                pltpu.roll(x_ref[r, c, :, t * rows : (t + 1) * rows].astype(f32), amount, 1)
                for t in range(bands)
            ]
            zero = jnp.zeros((chans, rows), f32)
            for t in range(bands):
                low = rolled[t - 1] if t else zero
                high = rolled[t + 1] if t + 1 < bands else zero
                out = jnp.where(pos < 0, low, jnp.where(pos >= rows, high, rolled[t]))
                o_ref[t, c, r] = out.astype(half)
        meta_ref[pl.ds(r, 1), :] = jnp.full((1, meta_ref.shape[1]), shifts[r, 1], jnp.int32)
        return carry

    lax.fori_loop(0, count, one, 0)


def gather_kernel(sizes, s_ref, m_ref, o_ref, mo_ref, loc, send1, recv1, send2, recv2, sendm, recvm):
    nrow, bands, passes = sizes
    p = lax.axis_index("pass")
    b = lax.axis_index("tile") * nrow + lax.axis_index("row")

    def band_id(k):
        return {"tile": k // nrow, "row": k % nrow}

    barrier = pltpu.get_barrier_semaphore()
    for k in range(1, bands):
        pl.semaphore_signal(
            barrier, inc=1, device_id=band_id((b + k) % bands), device_id_type=MESH
        )
    for k in range(1, passes):
        pl.semaphore_signal(
            barrier, inc=1, device_id={"pass": (p + k) % passes}, device_id_type=MESH
        )
    pl.semaphore_wait(barrier, bands + passes - 2)

    own = pltpu.make_async_copy(s_ref.at[b], o_ref.at[p, b], loc.at[0])
    own.start()
    own_meta = pltpu.make_async_copy(m_ref, mo_ref.at[p], loc.at[1])
    own_meta.start()
    pending = []

    def forward(src, slot, index):
        for k in range(1, passes):
            copy = pltpu.make_async_remote_copy(
                src_ref=src,
                dst_ref=o_ref.at[p, index],
                send_sem=send2.at[k - 1, slot],
                recv_sem=recv2.at[k - 1, slot],
                device_id={"pass": (p + k) % passes},
                device_id_type=MESH,
            )
            copy.start()
            pending.append(copy)

    for k in range(1, passes):
        copy = pltpu.make_async_remote_copy(
            src_ref=m_ref,
            dst_ref=mo_ref.at[p],
            send_sem=sendm.at[k - 1],
            recv_sem=recvm.at[k - 1],
            device_id={"pass": (p + k) % passes},
            device_id_type=MESH,
        )
        copy.start()
        pending.append(copy)
    forward(s_ref.at[b], 0, b)
    first = []
    order = [k for k in range(1, bands)]
    order.sort(key=lambda k: min(k, bands - k))
    for k in reversed(order):
        peer = (b + k) % bands
        copy = pltpu.make_async_remote_copy(
            src_ref=s_ref.at[peer],
            dst_ref=o_ref.at[p, b],
            send_sem=send1.at[k - 1],
            recv_sem=recv1.at[k - 1],
            device_id=band_id(peer),
            device_id_type=MESH,
        )
        copy.start()
        first.append((k, copy))
    for k, copy in first:
        copy.wait_recv()
        source = (b + bands - k) % bands
        forward(o_ref.at[p, source], k, source)
    for _, copy in first:
        copy.wait_send()
    for copy in pending:
        copy.wait()
    own.wait()
    own_meta.wait()


def rms(values, gain):
    mean = jnp.mean(values * values, axis=0, keepdims=True)
    return values * lax.rsqrt(mean + eps) * gain


QUAD = 4


def join_kernel(
    cols,
    meta,
    flags,
    x_ref,
    gains,
    spread,
    gather,
    w_query,
    w_key,
    w_value,
    w_out,
    w_in,
    w_back,
    o_ref,
    cells,
    q_s,
    k_s,
    v_s,
    total_s,
    picked,
):
    passes, ncols, per, chans, rows = x_ref.shape
    count = passes * per
    base = lax.axis_index("pass") * cols
    g1, gq, gk, g2 = (jnp.concatenate([gains[i], gains[i]], axis=1) for i in range(4))
    within = lax.broadcasted_iota(jnp.int32, (QUAD * HEADS, 2 * rows), 0) // HEADS
    flag_sum = jnp.int32(0)
    for s in range(count):
        flag_sum = flag_sum + flags[s, 0]
    k_s[...] = jnp.zeros_like(k_s)
    v_s[...] = jnp.zeros_like(v_s)

    def column(x, carry):
        live = jnp.int32(0)
        zeros = jnp.int32(0)
        for r in range(count):
            col = base + x + meta[r // per, r % per, 0]
            inside = ((col >= 0) & (col < ncols)).astype(jnp.int32)
            picked[live] = r
            live = live + inside * flags[r, 0]
            zeros = zeros + (1 - inside) * flags[r, 0]
        picked[live] = 0
        zeros = zeros.astype(f32)
        pairs = jnp.minimum((live + 2) // 2, count // 2)
        quads = (2 * pairs + QUAD - 1) // QUAD

        def weight_of(slot):
            return jnp.where(slot < live, 1.0, jnp.where(slot == live, zeros, 0.0))

        def project(j, carry):
            pair = []
            for i in range(2):
                slot = 2 * j + i
                r = picked[jnp.minimum(slot, live)]
                pr, rr = r // per, r % per
                col = jnp.clip(base + x + meta[pr, rr, 0], 0, ncols - 1)
                pair.append(jnp.where(slot < live, x_ref[pr, col, rr].astype(f32), 0.0))
            both = jnp.concatenate(pair, axis=1)
            cells[j] = both
            normed = rms(both, g1).astype(half)
            q_s[j] = rms(dot_t(w_query[...], normed), gq).astype(half)
            k_hat = rms(dot_t(w_key[...], normed), gk).astype(half)
            value = dot_t(w_value[...], normed).astype(half).astype(f32)
            for i in range(2):
                k_s[2 * j + i] = k_hat[:, i * rows : (i + 1) * rows]
                v_s[2 * j + i] = value[:, i * rows : (i + 1) * rows]
            return carry

        lax.fori_loop(0, pairs, project, 0)
        total_s[...] = jnp.zeros_like(total_s)

        def attend(j, carry):
            q_pair = q_s[j]

            def keys_of(k, sums):
                above, below = sums
                keys = k_s[pl.ds(QUAD * k, QUAD)]
                prods = [
                    (keys * q_pair[:, i * rows : (i + 1) * rows][None]).reshape(QUAD * chans, rows)
                    for i in range(2)
                ]
                scores = jnp.dot(
                    spread[...], jnp.concatenate(prods, axis=1), preferred_element_type=f32
                )
                weights = (jnp.exp(scores) * weight_of(within + QUAD * k)).astype(half)
                wide = jnp.dot(gather[...], weights, preferred_element_type=f32)
                for s in range(QUAD):
                    part = wide[s * chans : (s + 1) * chans]
                    value = v_s[QUAD * k + s]
                    above = above + part * jnp.concatenate([value, value], axis=1)
                    below = below + part
                return above, below

            zero = jnp.zeros((chans, 2 * rows), f32)
            above, below = lax.fori_loop(0, quads, keys_of, (zero, zero))
            mixed = (above / below).astype(half)
            hidden = cells[j] + dot_t(w_out[...], mixed)
            normed = rms(hidden, g2).astype(half)
            inner = jax.nn.gelu(dot_t(w_in[...], normed), approximate=True).astype(half)
            tokens = hidden + dot_t(w_back[...], inner)
            total_s[...] += tokens[:, :rows] * weight_of(2 * j) + tokens[:, rows:] * weight_of(
                2 * j + 1
            )
            return carry

        lax.fori_loop(0, pairs, attend, 0)
        o_ref[x] = (total_s[...] / flag_sum.astype(f32)).astype(half)
        return carry

    lax.fori_loop(0, cols, column, 0)


MOVES = [(dp, db) for dp in (-1, 0, 1) for db in (-1, 0, 1) if (dp, db) != (0, 0)]


def decode_kernel(sizes, j_ref, w1, w2, o_ref, *scratch):
    nrow, bands, passes = sizes
    bufs = scratch[: len(MOVES)]
    taps, acts, send, recv = scratch[len(MOVES) :]
    cols, chans, rows = j_ref.shape
    p = lax.axis_index("pass")
    b = lax.axis_index("tile") * nrow + lax.axis_index("row")

    def exists(dp, db):
        ok = jnp.bool_(True)
        if dp:
            ok = ok & (p + dp >= 0) & (p + dp < passes)
        if db:
            ok = ok & (b + db >= 0) & (b + db < bands)
        return ok

    def target(dp, db):
        k = b + db
        return {"pass": p + dp, "tile": k // nrow, "row": k % nrow}

    barrier = pltpu.get_barrier_semaphore()
    neighbours = jnp.int32(0)
    for dp, db in MOVES:
        there = exists(dp, db)
        neighbours = neighbours + there.astype(jnp.int32)

        @pl.when(there)
        def _():
            pl.semaphore_signal(barrier, inc=1, device_id=target(dp, db), device_id_type=MESH)

    pl.semaphore_wait(barrier, neighbours)

    def copy_of(n):
        dp, db = MOVES[n]
        src = j_ref
        if dp:
            src = j_ref.at[pl.ds(cols - 2 if dp > 0 else 0, 2)]
        return pltpu.make_async_remote_copy(
            src_ref=src,
            dst_ref=bufs[n],
            send_sem=send.at[n],
            recv_sem=recv.at[n],
            device_id=target(dp, db),
            device_id_type=MESH,
        )

    for n, (dp, db) in enumerate(MOVES):

        @pl.when(exists(dp, db))
        def _():
            copy_of(n).start()

    for n, (dp, db) in enumerate(MOVES):

        @pl.when(exists(-dp, -db))
        def _():
            copy_of(n).wait_recv()

        @pl.when(jnp.logical_not(exists(-dp, -db)))
        def _():
            bufs[n][...] = jnp.zeros_like(bufs[n])

    def side(dp, db):
        return bufs[MOVES.index((-dp, -db))]

    lane = lax.broadcasted_iota(jnp.int32, (chans, rows), 1)
    wide_lane = lax.broadcasted_iota(jnp.int32, (chans, 2 * rows), 1)

    def widen(values):
        last = 2 * rows - 1
        return jnp.concatenate(
            [
                pltpu.roll(values, 1, 1).astype(half),
                values.astype(half),
                pltpu.roll(values, last, 1).astype(half),
            ],
            axis=0,
        )

    for n in range(cols + 4):
        dp = -1 if n < 2 else (1 if n >= cols + 2 else 0)
        at = n if dp < 0 else (n - cols - 2 if dp > 0 else n - 2)
        middle = j_ref[at] if dp == 0 else side(dp, 0)[at]
        border = jnp.where(
            lane < rows // 2, side(dp, 1)[at].astype(f32), side(dp, -1)[at].astype(f32)
        )
        taps[n] = widen(jnp.concatenate([middle.astype(f32), border], axis=1))
    row_pos = b * rows + jnp.where(wide_lane < rows + rows // 2, wide_lane, wide_lane - 2 * rows)
    row_inside = (row_pos >= 0) & (row_pos < bands * rows)
    for n in range(cols + 2):
        near = taps[n : n + 3].reshape(9 * chans, 2 * rows)
        act = jax.nn.gelu(dot_t(w1[...], near), approximate=True)
        col_pos = p * cols + n - 1
        inside = row_inside & (col_pos >= 0) & (col_pos < passes * cols)
        acts[n] = widen(jnp.where(inside, act, 0.0))
    for n in range(cols):
        near = acts[n : n + 3, :, :rows].reshape(9 * chans, rows)
        o_ref[n] = dot_t(w2[...], near)

    for n, (dp, db) in enumerate(MOVES):

        @pl.when(exists(dp, db))
        def _():
            copy_of(n).wait_send()


def local(
    nrow,
    bands,
    passes,
    revisits,
    shifts,
    flags,
    norm1_gain,
    w_query,
    w_key,
    w_value,
    query_gain,
    key_gain,
    w_out,
    norm2_gain,
    w_in,
    w_back,
    conv_first,
    conv_second,
):
    sizes = (nrow, bands, passes)
    per, own_cols, chans, all_rows = revisits.shape
    rows = all_rows // bands
    ncols = own_cols * bands
    cols = ncols // passes
    count = per * passes
    side_effects = dict(has_side_effects=True, vmem_limit_bytes=GRANT)
    shifted, meta = pl.pallas_call(
        shift_kernel,
        out_shape=(
            jax.ShapeDtypeStruct((bands, own_cols, per, chans, rows), half),
            jax.ShapeDtypeStruct((per, 128), jnp.int32),
        ),
        in_specs=[whole(pltpu.SMEM), whole()],
        out_specs=(whole(), whole()),
        compiler_params=pltpu.CompilerParams(vmem_limit_bytes=GRANT),
        name="row_shift",
    )(shifts, revisits)
    dma = pltpu.SemaphoreType.DMA
    others = max(passes - 1, 1)
    banded, metas = pl.pallas_call(
        functools.partial(gather_kernel, sizes),
        out_shape=(
            jax.ShapeDtypeStruct((passes, bands, own_cols, per, chans, rows), half),
            jax.ShapeDtypeStruct((passes, per, 128), jnp.int32),
        ),
        in_specs=[whole(), whole()],
        out_specs=(whole(), whole()),
        scratch_shapes=[
            dma((2,)),
            dma((bands,)),
            dma((bands,)),
            dma((others, bands)),
            dma((others, bands)),
            dma((others,)),
            dma((others,)),
        ],
        compiler_params=pltpu.CompilerParams(collective_id=0, **side_effects),
        name="exchange",
    )(shifted, meta)
    banded = banded.reshape(passes, ncols, per, chans, rows)
    gains = jnp.broadcast_to(
        jnp.stack([norm1_gain, query_gain, key_gain, norm2_gain])[:, :, None], (4, chans, rows)
    )
    head_size = chans // HEADS
    slots, heads = np.divmod(np.arange(QUAD * HEADS), HEADS)
    at = np.arange(QUAD * chans)
    match = (slots[:, None] == at[None] // chans) & (heads[:, None] == at[None] % chans // head_size)
    spread = jnp.asarray(match * (1.0 / math.sqrt(head_size)), half)
    gather = jnp.asarray(match.T, half)
    joined = pl.pallas_call(
        functools.partial(join_kernel, cols),
        out_shape=jax.ShapeDtypeStruct((cols, chans, rows), half),
        in_specs=[whole(pltpu.SMEM), whole(pltpu.SMEM)] + [whole()] * 10,
        out_specs=whole(),
        scratch_shapes=[
            pltpu.VMEM((count // 2, chans, 2 * rows), f32),
            pltpu.VMEM((count // 2, chans, 2 * rows), half),
            pltpu.VMEM((count, chans, rows), half),
            pltpu.VMEM((count, chans, rows), f32),
            pltpu.VMEM((chans, rows), f32),
            pltpu.SMEM((count + 1,), jnp.int32),
        ],
        compiler_params=pltpu.CompilerParams(vmem_limit_bytes=GRANT),
        name="join",
    )(metas, flags, banded, gains, spread, gather, w_query, w_key, w_value, w_out, w_in, w_back)
    outs = conv_second.shape[3]
    return pl.pallas_call(
        functools.partial(decode_kernel, sizes),
        out_shape=jax.ShapeDtypeStruct((cols, outs, rows), f32),
        in_specs=[whole()] * 3,
        out_specs=whole(),
        scratch_shapes=[
            pltpu.VMEM((2 if dp else cols, chans, rows), half) for dp, db in MOVES
        ]
        + [
            pltpu.VMEM((cols + 4, 3 * chans, 2 * rows), half),
            pltpu.VMEM((cols + 2, 3 * chans, 2 * rows), half),
            dma((len(MOVES),)),
            dma((len(MOVES),)),
        ],
        compiler_params=pltpu.CompilerParams(collective_id=1, **side_effects),
        name="decode",
    )(joined, conv_first.reshape(9 * chans, -1), conv_second.reshape(9 * chans, outs))


def solution(mesh):
    shape = mesh.shape
    fixed = [P()] * 12
    return jax.shard_map(
        functools.partial(local, shape["row"], shape["tile"] * shape["row"], shape["pass"]),
        mesh=mesh,
        in_specs=(
            P(("groups", "pass"), ("tile", "row"), None, None),
            P(("groups", "pass"), None),
            P("groups", ("tile", "row")),
            *fixed,
        ),
        out_specs=P(("groups", "pass"), None, ("tile", "row")),
        check_vma=False,
    )
```

```python
import functools
import math

import jax
import jax.numpy as jnp
import numpy as np
from jax import lax
from jax.experimental import pallas as pl
from jax.experimental.pallas import tpu as pltpu
from jax.sharding import PartitionSpec as P

HEADS = 4
eps = 1e-05
f32 = jnp.float32
half = jnp.bfloat16
MESH = pl.DeviceIdType.MESH
GRANT = 60 * 1024 * 1024


def whole(space=pltpu.VMEM):
    return pl.BlockSpec(memory_space=space)


def dot_t(weights, values):
    return lax.dot_general(
        weights, values, (((0,), (0,)), ((), ())), preferred_element_type=f32
    )


def census_kernel(sizes, ncols, s_ref, mo_ref, peak_ref, held, send, recv):
    groups, passes = sizes
    total = groups * passes
    g = lax.axis_index("groups")
    me = g * passes + lax.axis_index("pass")

    def peer(k):
        k = (me + k) % total
        return {"groups": k // passes, "pass": k % passes}

    barrier = pltpu.get_barrier_semaphore()
    for k in range(1, total):
        pl.semaphore_signal(barrier, inc=1, device_id=peer(k), device_id_type=MESH)
    pl.semaphore_wait(barrier, total - 1)
    copies = []
    for k in range(1, total):
        copy = pltpu.make_async_remote_copy(
            src_ref=s_ref,
            dst_ref=held.at[me],
            send_sem=send.at[k - 1],
            recv_sem=recv.at[k - 1],
            device_id=peer(k),
            device_id_type=MESH,
        )
        copy.start()
        copies.append(copy)
    held[me] = s_ref[...]
    for copy in copies:
        copy.wait()
    per = s_ref.shape[0]
    lane = lax.broadcasted_iota(jnp.int32, (per, peak_ref.shape[1]), 1)
    peak = jnp.zeros((1, peak_ref.shape[1]), f32)
    for k in range(total):
        col = lane - held[k][:, 1:2]
        needed = jnp.where((col >= 0) & (col < ncols) & (lane < ncols), 1.0, 0.0)
        peak = jnp.maximum(peak, jnp.sum(needed, axis=0, keepdims=True))
    peak = jnp.max(peak, axis=1, keepdims=True)
    peak_ref[...] = jnp.broadcast_to(peak, peak_ref.shape)
    for k in range(passes):
        mo_ref[k] = held[g * passes + k]


def shift_kernel(sizes, shifts, x_ref, o_ref):
    nrow, ncols = sizes
    bands, per, count, chans, rows = o_ref.shape
    lane = lax.broadcasted_iota(jnp.int32, (chans, rows), 1)
    b = lax.axis_index("tile") * nrow + lax.axis_index("row")
    for c in range(per):

        def one(r, slot, c=c):
            col = b * per + c - shifts[r, 1]
            needed = (col >= 0) & (col < ncols)

            @pl.when(needed)
            def _():
                offset = shifts[r, 0]
                amount = lax.rem(2 * rows - offset, rows)
                pos = lane + offset
                rolled = [
                    pltpu.roll(x_ref[r, c, :, t * rows : (t + 1) * rows].astype(f32), amount, 1)
                    for t in range(bands)
                ]
                zero = jnp.zeros((chans, rows), f32)
                for t in range(bands):
                    low = rolled[t - 1] if t else zero
                    high = rolled[t + 1] if t + 1 < bands else zero
                    out = jnp.where(pos < 0, low, jnp.where(pos >= rows, high, rolled[t]))
                    o_ref[t, c, slot] = out.astype(half)

            return slot + needed.astype(jnp.int32)

        lax.fori_loop(0, count, one, 0)


def gather_kernel(sizes, slots, s_ref, o_ref, loc, send1, recv1, send2, recv2):
    nrow, bands, passes = sizes
    p = lax.axis_index("pass")
    b = lax.axis_index("tile") * nrow + lax.axis_index("row")

    def band_id(k):
        return {"tile": k // nrow, "row": k % nrow}

    def used(*at):
        return at + (slice(None), pl.ds(0, slots))

    barrier = pltpu.get_barrier_semaphore()
    for k in range(1, bands):
        pl.semaphore_signal(
            barrier, inc=1, device_id=band_id((b + k) % bands), device_id_type=MESH
        )
    for k in range(1, passes):
        pl.semaphore_signal(
            barrier, inc=1, device_id={"pass": (p + k) % passes}, device_id_type=MESH
        )
    pl.semaphore_wait(barrier, bands + passes - 2)

    own = pltpu.make_async_copy(s_ref.at[used(b)], o_ref.at[used(p, b)], loc.at[0])
    own.start()
    pending = []

    def forward(src, slot, index):
        for k in range(1, passes):
            copy = pltpu.make_async_remote_copy(
                src_ref=src,
                dst_ref=o_ref.at[used(p, index)],
                send_sem=send2.at[k - 1, slot],
                recv_sem=recv2.at[k - 1, slot],
                device_id={"pass": (p + k) % passes},
                device_id_type=MESH,
            )
            copy.start()
            pending.append(copy)

    forward(s_ref.at[used(b)], 0, b)
    first = []
    order = [k for k in range(1, bands)]
    order.sort(key=lambda k: min(k, bands - k))
    for k in reversed(order):
        peer = (b + k) % bands
        copy = pltpu.make_async_remote_copy(
            src_ref=s_ref.at[used(peer)],
            dst_ref=o_ref.at[used(p, b)],
            send_sem=send1.at[k - 1],
            recv_sem=recv1.at[k - 1],
            device_id=band_id(peer),
            device_id_type=MESH,
        )
        copy.start()
        first.append((k, copy))
    for k, copy in first:
        copy.wait_recv()
        source = (b + bands - k) % bands
        forward(o_ref.at[used(p, source)], k, source)
    for _, copy in first:
        copy.wait_send()
    for copy in pending:
        copy.wait()
    own.wait()


def rms(values, gain):
    mean = jnp.mean(values * values, axis=0, keepdims=True)
    return values * lax.rsqrt(mean + eps) * gain


QUAD = 4


def join_kernel(
    cols,
    ncols,
    meta,
    flags,
    x_ref,
    gains,
    spread,
    gather,
    w_query,
    w_key,
    w_value,
    w_out,
    w_in,
    w_back,
    o_ref,
    cells,
    q_s,
    k_s,
    v_s,
    w_s,
    total_s,
    picked,
):
    passes, per, _ = meta.shape
    chans, rows = x_ref.shape[1:]
    count = passes * per
    base = lax.axis_index("pass") * cols
    g1, gq, gk, g2 = (jnp.concatenate([gains[i], gains[i]], axis=1) for i in range(4))
    within = lax.broadcasted_iota(jnp.int32, (QUAD * HEADS, 2 * rows), 0) // HEADS
    flag_sum = jnp.int32(0)
    for s in range(count):
        flag_sum = flag_sum + flags[s, 0]
    k_s[...] = jnp.zeros_like(k_s)
    v_s[...] = jnp.zeros_like(v_s)

    def column(x, carry):
        live = jnp.int32(0)
        zeros = jnp.int32(0)
        for r in range(count):
            col = base + x + meta[r // per, r % per, 1]
            inside = ((col >= 0) & (col < ncols)).astype(jnp.int32)

            @pl.when(inside * flags[r, 0] == 1)
            def _(r=r, col=col, live=live):
                slot = jnp.int32(0)
                for other in range(r % per):
                    to = col - meta[r // per, other, 1]
                    slot = slot + ((to >= 0) & (to < ncols)).astype(jnp.int32)
                picked[live] = (r // per * ncols + col) * per + slot

            live = live + inside * flags[r, 0]
            zeros = zeros + (1 - inside) * flags[r, 0]
        picked[live] = 0
        zeros = zeros.astype(f32)
        pairs = jnp.minimum((live + 2) // 2, count // 2)
        quads = (2 * pairs + QUAD - 1) // QUAD

        def weight_of(slot):
            return jnp.where(slot < live, 1.0, jnp.where(slot == live, zeros, 0.0))

        def project(j, carry):
            pair = []
            for i in range(2):
                slot = 2 * j + i
                value = x_ref[picked[jnp.minimum(slot, live)]].astype(f32)
                pair.append(jnp.where(slot < live, value, 0.0))
            both = jnp.concatenate(pair, axis=1)
            cells[j] = both
            normed = rms(both, g1).astype(half)
            q_s[j] = rms(dot_t(w_query[...], normed), gq).astype(half)
            k_hat = rms(dot_t(w_key[...], normed), gk).astype(half)
            value = dot_t(w_value[...], normed).astype(half).astype(f32)
            for i in range(2):
                k_s[2 * j + i] = k_hat[:, i * rows : (i + 1) * rows]
                v_s[2 * j + i] = value[:, i * rows : (i + 1) * rows]
            return carry

        lax.fori_loop(0, pairs, project, 0)
        total_s[...] = jnp.zeros_like(total_s)

        def attend(j, carry):
            q_pair = q_s[j]

            def keys_of(k, below):
                keys = k_s[pl.ds(QUAD * k, QUAD)]
                prods = [
                    (keys * q_pair[:, i * rows : (i + 1) * rows][None]).reshape(QUAD * chans, rows)
                    for i in range(2)
                ]
                scores = jnp.dot(
                    spread[...], jnp.concatenate(prods, axis=1), preferred_element_type=f32
                )
                weights = jnp.exp(scores) * weight_of(within + QUAD * k)
                w_s[k] = weights
                return below + weights[:8] + weights[8:]

            below = lax.fori_loop(0, quads, keys_of, jnp.zeros((8, 2 * rows), f32))
            below = below + pltpu.roll(below, HEADS, 0)
            below = jnp.concatenate([below, below], axis=0)

            def values_of(k, above):
                probs = (w_s[k] / below).astype(half)
                wide = jnp.dot(gather[...], probs, preferred_element_type=f32)
                for s in range(QUAD):
                    value = v_s[QUAD * k + s]
                    above = above + wide[s * chans : (s + 1) * chans] * jnp.concatenate(
                        [value, value], axis=1
                    )
                return above

            above = lax.fori_loop(0, quads, values_of, jnp.zeros((chans, 2 * rows), f32))
            mixed = above.astype(half)
            hidden = cells[j] + dot_t(w_out[...], mixed)
            normed = rms(hidden, g2).astype(half)
            inner = jax.nn.gelu(dot_t(w_in[...], normed), approximate=True).astype(half)
            tokens = hidden + dot_t(w_back[...], inner)
            total_s[...] += tokens[:, :rows] * weight_of(2 * j) + tokens[:, rows:] * weight_of(
                2 * j + 1
            )
            return carry

        lax.fori_loop(0, pairs, attend, 0)
        o_ref[x] = (total_s[...] / flag_sum.astype(f32)).astype(half)
        return carry

    lax.fori_loop(0, cols, column, 0)


MOVES = [(dp, db) for dp in (-1, 0, 1) for db in (-1, 0, 1) if (dp, db) != (0, 0)]


def decode_kernel(sizes, j_ref, w1, w2, o_ref, *scratch):
    nrow, bands, passes = sizes
    bufs = scratch[: len(MOVES)]
    taps, acts, send, recv = scratch[len(MOVES) :]
    cols, chans, rows = j_ref.shape
    p = lax.axis_index("pass")
    b = lax.axis_index("tile") * nrow + lax.axis_index("row")

    def exists(dp, db):
        ok = jnp.bool_(True)
        if dp:
            ok = ok & (p + dp >= 0) & (p + dp < passes)
        if db:
            ok = ok & (b + db >= 0) & (b + db < bands)
        return ok

    def target(dp, db):
        k = b + db
        return {"pass": p + dp, "tile": k // nrow, "row": k % nrow}

    barrier = pltpu.get_barrier_semaphore()
    neighbours = jnp.int32(0)
    for dp, db in MOVES:
        there = exists(dp, db)
        neighbours = neighbours + there.astype(jnp.int32)

        @pl.when(there)
        def _():
            pl.semaphore_signal(barrier, inc=1, device_id=target(dp, db), device_id_type=MESH)

    pl.semaphore_wait(barrier, neighbours)

    def copy_of(n):
        dp, db = MOVES[n]
        src = j_ref
        if dp:
            src = j_ref.at[pl.ds(cols - 2 if dp > 0 else 0, 2)]
        return pltpu.make_async_remote_copy(
            src_ref=src,
            dst_ref=bufs[n],
            send_sem=send.at[n],
            recv_sem=recv.at[n],
            device_id=target(dp, db),
            device_id_type=MESH,
        )

    for n, (dp, db) in enumerate(MOVES):

        @pl.when(exists(dp, db))
        def _():
            copy_of(n).start()

    for n, (dp, db) in enumerate(MOVES):

        @pl.when(exists(-dp, -db))
        def _():
            copy_of(n).wait_recv()

        @pl.when(jnp.logical_not(exists(-dp, -db)))
        def _():
            bufs[n][...] = jnp.zeros_like(bufs[n])

    def side(dp, db):
        return bufs[MOVES.index((-dp, -db))]

    lane = lax.broadcasted_iota(jnp.int32, (chans, rows), 1)
    wide_lane = lax.broadcasted_iota(jnp.int32, (chans, 2 * rows), 1)

    def widen(values):
        last = 2 * rows - 1
        return jnp.concatenate(
            [
                pltpu.roll(values, 1, 1).astype(half),
                values.astype(half),
                pltpu.roll(values, last, 1).astype(half),
            ],
            axis=0,
        )

    for n in range(cols + 4):
        dp = -1 if n < 2 else (1 if n >= cols + 2 else 0)
        at = n if dp < 0 else (n - cols - 2 if dp > 0 else n - 2)
        middle = j_ref[at] if dp == 0 else side(dp, 0)[at]
        border = jnp.where(
            lane < rows // 2, side(dp, 1)[at].astype(f32), side(dp, -1)[at].astype(f32)
        )
        taps[n] = widen(jnp.concatenate([middle.astype(f32), border], axis=1))
    row_pos = b * rows + jnp.where(wide_lane < rows + rows // 2, wide_lane, wide_lane - 2 * rows)
    row_inside = (row_pos >= 0) & (row_pos < bands * rows)
    for n in range(cols + 2):
        near = taps[n : n + 3].reshape(9 * chans, 2 * rows)
        act = jax.nn.gelu(dot_t(w1[...], near), approximate=True)
        col_pos = p * cols + n - 1
        inside = row_inside & (col_pos >= 0) & (col_pos < passes * cols)
        acts[n] = widen(jnp.where(inside, act, 0.0))
    for n in range(cols):
        near = acts[n : n + 3, :, :rows].reshape(9 * chans, rows)
        o_ref[n] = dot_t(w2[...], near)

    for n, (dp, db) in enumerate(MOVES):

        @pl.when(exists(dp, db))
        def _():
            copy_of(n).wait_send()


def local(
    groups,
    nrow,
    bands,
    passes,
    revisits,
    shifts,
    flags,
    norm1_gain,
    w_query,
    w_key,
    w_value,
    query_gain,
    key_gain,
    w_out,
    norm2_gain,
    w_in,
    w_back,
    conv_first,
    conv_second,
):
    sizes = (nrow, bands, passes)
    per, own_cols, chans, all_rows = revisits.shape
    rows = all_rows // bands
    ncols = own_cols * bands
    cols = ncols // passes
    count = per * passes
    side_effects = dict(has_side_effects=True, vmem_limit_bytes=GRANT)
    dma = pltpu.SemaphoreType.DMA
    total = groups * passes
    metas, peak = pl.pallas_call(
        functools.partial(census_kernel, (groups, passes), ncols),
        out_shape=(
            jax.ShapeDtypeStruct((passes, per, 2), jnp.int32),
            jax.ShapeDtypeStruct((8, 128), f32),
        ),
        in_specs=[whole()],
        out_specs=(whole(), whole()),
        scratch_shapes=[
            pltpu.VMEM((total, per, 2), jnp.int32),
            dma((max(total - 1, 1),)),
            dma((max(total - 1, 1),)),
        ],
        compiler_params=pltpu.CompilerParams(collective_id=0, **side_effects),
        name="census",
    )(shifts)
    shifted = pl.pallas_call(
        functools.partial(shift_kernel, (nrow, ncols)),
        out_shape=jax.ShapeDtypeStruct((bands, own_cols, per, chans, rows), half),
        in_specs=[whole(pltpu.SMEM), whole()],
        out_specs=whole(),
        compiler_params=pltpu.CompilerParams(vmem_limit_bytes=GRANT),
        name="row_shift",
    )(shifts, revisits)
    others = max(passes - 1, 1)
    levels = sorted({min(k, per) for k in (2, 3, 4, per)})

    def exchange(index):
        return pl.pallas_call(
            functools.partial(gather_kernel, sizes, levels[index]),
            out_shape=jax.ShapeDtypeStruct((passes, bands, own_cols, per, chans, rows), half),
            in_specs=[whole()],
            out_specs=whole(pl.ANY),
            scratch_shapes=[
                dma((1,)),
                dma((bands,)),
                dma((bands,)),
                dma((others, bands)),
                dma((others, bands)),
            ],
            compiler_params=pltpu.CompilerParams(collective_id=2 + index, **side_effects),
            name="exchange",
        )

    level = sum((peak[0, 0] > k).astype(jnp.int32) for k in levels[:-1]) + jnp.int32(0)
    banded = lax.switch(level, [exchange(i) for i in range(len(levels))], shifted)
    banded = banded.reshape(passes * ncols * per, chans, rows)
    gains = jnp.broadcast_to(
        jnp.stack([norm1_gain, query_gain, key_gain, norm2_gain])[:, :, None], (4, chans, rows)
    )
    head_size = chans // HEADS
    slots, heads = np.divmod(np.arange(QUAD * HEADS), HEADS)
    at = np.arange(QUAD * chans)
    match = (slots[:, None] == at[None] // chans) & (heads[:, None] == at[None] % chans // head_size)
    spread = jnp.asarray(match * (1.0 / math.sqrt(head_size)), half)
    gather = jnp.asarray(match.T, half)
    joined = pl.pallas_call(
        functools.partial(join_kernel, cols, ncols),
        out_shape=jax.ShapeDtypeStruct((cols, chans, rows), half),
        in_specs=[whole(pltpu.SMEM), whole(pltpu.SMEM)] + [whole()] * 10,
        out_specs=whole(),
        scratch_shapes=[
            pltpu.VMEM((count // 2, chans, 2 * rows), f32),
            pltpu.VMEM((count // 2, chans, 2 * rows), half),
            pltpu.VMEM((count, chans, rows), half),
            pltpu.VMEM((count, chans, rows), f32),
            pltpu.VMEM((count // QUAD, QUAD * HEADS, 2 * rows), f32),
            pltpu.VMEM((chans, rows), f32),
            pltpu.SMEM((count + 1,), jnp.int32),
        ],
        compiler_params=pltpu.CompilerParams(vmem_limit_bytes=GRANT),
        name="join",
    )(metas, flags, banded, gains, spread, gather, w_query, w_key, w_value, w_out, w_in, w_back)
    outs = conv_second.shape[3]
    return pl.pallas_call(
        functools.partial(decode_kernel, sizes),
        out_shape=jax.ShapeDtypeStruct((cols, outs, rows), f32),
        in_specs=[whole()] * 3,
        out_specs=whole(),
        scratch_shapes=[
            pltpu.VMEM((2 if dp else cols, chans, rows), half) for dp, db in MOVES
        ]
        + [
            pltpu.VMEM((cols + 4, 3 * chans, 2 * rows), half),
            pltpu.VMEM((cols + 2, 3 * chans, 2 * rows), half),
            dma((len(MOVES),)),
            dma((len(MOVES),)),
        ],
        compiler_params=pltpu.CompilerParams(collective_id=1, **side_effects),
        name="decode",
    )(joined, conv_first.reshape(9 * chans, -1), conv_second.reshape(9 * chans, outs))


def solution(mesh):
    shape = mesh.shape
    fixed = [P()] * 12
    return jax.shard_map(
        functools.partial(local, shape["groups"], shape["row"], shape["tile"] * shape["row"], shape["pass"]),
        mesh=mesh,
        in_specs=(
            P(("groups", "pass"), ("tile", "row"), None, None),
            P(("groups", "pass"), None),
            P("groups", ("tile", "row")),
            *fixed,
        ),
        out_specs=P(("groups", "pass"), None, ("tile", "row")),
        check_vma=False,
    )
```

```python
import functools
import math

import jax
import jax.numpy as jnp
import numpy as np
from jax import lax
from jax.experimental import pallas as pl
from jax.experimental.pallas import tpu as pltpu
from jax.sharding import PartitionSpec as P

HEADS = 4
eps = 1e-05
f32 = jnp.float32
half = jnp.bfloat16
MESH = pl.DeviceIdType.MESH
GRANT = 60 * 1024 * 1024


def whole(space=pltpu.VMEM):
    return pl.BlockSpec(memory_space=space)


def dot_t(weights, values):
    return lax.dot_general(
        weights, values, (((0,), (0,)), ((), ())), preferred_element_type=f32
    )


def census_kernel(sizes, ncols, s_ref, mo_ref, level_ref, held, send, recv):
    groups, passes = sizes
    total = groups * passes
    g = lax.axis_index("groups")
    me = g * passes + lax.axis_index("pass")

    def peer(k):
        k = (me + k) % total
        return {"groups": k // passes, "pass": k % passes}

    barrier = pltpu.get_barrier_semaphore()
    for k in range(1, total):
        pl.semaphore_signal(barrier, inc=1, device_id=peer(k), device_id_type=MESH)
    pl.semaphore_wait(barrier, total - 1)
    copies = []
    for k in range(1, total):
        copy = pltpu.make_async_remote_copy(
            src_ref=s_ref,
            dst_ref=held.at[me],
            send_sem=send.at[k - 1],
            recv_sem=recv.at[k - 1],
            device_id=peer(k),
            device_id_type=MESH,
        )
        copy.start()
        copies.append(copy)
    held[me] = s_ref[...]
    for copy in copies:
        copy.wait()
    per = s_ref.shape[1]
    source = lax.broadcasted_iota(jnp.int32, (ncols, per), 0)
    peak = jnp.zeros((ncols, 1), f32)
    for k in range(total):
        col = source - held[k][1:2, :]
        needed = jnp.where((col >= 0) & (col < ncols), 1.0, 0.0)
        peak = jnp.maximum(peak, jnp.sum(needed, axis=1, keepdims=True))
    level_ref[0] = jnp.max(peak).astype(jnp.int32)
    for k in range(passes):
        mo_ref[k] = held[g * passes + k]


def shift_kernel(sizes, shifts, x_ref, o_ref):
    nrow, ncols = sizes
    bands, per, count, chans, rows = o_ref.shape
    lane = lax.broadcasted_iota(jnp.int32, (chans, rows), 1)
    b = lax.axis_index("tile") * nrow + lax.axis_index("row")
    for c in range(per):

        def one(r, slot, c=c):
            col = b * per + c - shifts[1, r]
            needed = (col >= 0) & (col < ncols)

            @pl.when(needed)
            def _():
                offset = shifts[0, r]
                amount = lax.rem(2 * rows - offset, rows)
                pos = lane + offset
                rolled = [
                    pltpu.roll(x_ref[r, c, :, t * rows : (t + 1) * rows].astype(f32), amount, 1)
                    for t in range(bands)
                ]
                zero = jnp.zeros((chans, rows), f32)
                for t in range(bands):
                    low = rolled[t - 1] if t else zero
                    high = rolled[t + 1] if t + 1 < bands else zero
                    out = jnp.where(pos < 0, low, jnp.where(pos >= rows, high, rolled[t]))
                    o_ref[t, c, slot] = out.astype(half)

            return slot + needed.astype(jnp.int32)

        lax.fori_loop(0, count, one, 0)


def gather_kernel(sizes, slots, s_ref, o_ref, loc, send1, recv1, send2, recv2):
    nrow, bands, passes = sizes
    p = lax.axis_index("pass")
    b = lax.axis_index("tile") * nrow + lax.axis_index("row")

    def band_id(k):
        return {"tile": k // nrow, "row": k % nrow}

    def used(*at):
        return at + (slice(None), pl.ds(0, slots))

    barrier = pltpu.get_barrier_semaphore()
    for k in range(1, bands):
        pl.semaphore_signal(
            barrier, inc=1, device_id=band_id((b + k) % bands), device_id_type=MESH
        )
    for k in range(1, passes):
        pl.semaphore_signal(
            barrier, inc=1, device_id={"pass": (p + k) % passes}, device_id_type=MESH
        )
    pl.semaphore_wait(barrier, bands + passes - 2)

    own = pltpu.make_async_copy(s_ref.at[used(b)], o_ref.at[used(p, b)], loc.at[0])
    own.start()
    pending = []

    def forward(src, slot, index):
        for k in range(1, passes):
            copy = pltpu.make_async_remote_copy(
                src_ref=src,
                dst_ref=o_ref.at[used(p, index)],
                send_sem=send2.at[k - 1, slot],
                recv_sem=recv2.at[k - 1, slot],
                device_id={"pass": (p + k) % passes},
                device_id_type=MESH,
            )
            copy.start()
            pending.append(copy)

    forward(s_ref.at[used(b)], 0, b)
    first = []
    order = [k for k in range(1, bands)]
    order.sort(key=lambda k: min(k, bands - k))
    for k in reversed(order):
        peer = (b + k) % bands
        copy = pltpu.make_async_remote_copy(
            src_ref=s_ref.at[used(peer)],
            dst_ref=o_ref.at[used(p, b)],
            send_sem=send1.at[k - 1],
            recv_sem=recv1.at[k - 1],
            device_id=band_id(peer),
            device_id_type=MESH,
        )
        copy.start()
        first.append((k, copy))
    for k, copy in first:
        copy.wait_recv()
        source = (b + bands - k) % bands
        forward(o_ref.at[used(p, source)], k, source)
    for _, copy in first:
        copy.wait_send()
    for copy in pending:
        copy.wait()
    own.wait()


def rms(values, gain):
    mean = jnp.mean(values * values, axis=0, keepdims=True)
    return values * lax.rsqrt(mean + eps) * gain


QUAD = 4


def join_kernel(
    cols,
    ncols,
    meta,
    flags,
    x_ref,
    gains,
    spread,
    gather,
    w_query,
    w_key,
    w_value,
    w_out,
    w_in,
    w_back,
    o_ref,
    cells,
    q_s,
    k_s,
    v_s,
    w_s,
    total_s,
    picked,
):
    passes, _, per = meta.shape
    chans, rows = x_ref.shape[1:]
    count = passes * per
    base = lax.axis_index("pass") * cols
    g1, gq, gk, g2 = (jnp.concatenate([gains[i], gains[i]], axis=1) for i in range(4))
    within = lax.broadcasted_iota(jnp.int32, (QUAD * HEADS, 2 * rows), 0) // HEADS
    flag_sum = jnp.int32(0)
    for s in range(count):
        flag_sum = flag_sum + flags[0, s]
    k_s[...] = jnp.zeros_like(k_s)
    v_s[...] = jnp.zeros_like(v_s)

    def column(x, carry):
        live = jnp.int32(0)
        zeros = jnp.int32(0)
        for r in range(count):
            col = base + x + meta[r // per, 1, r % per]
            inside = ((col >= 0) & (col < ncols)).astype(jnp.int32)

            @pl.when(inside * flags[0, r] == 1)
            def _(r=r, col=col, live=live):
                slot = jnp.int32(0)
                for other in range(r % per):
                    to = col - meta[r // per, 1, other]
                    slot = slot + ((to >= 0) & (to < ncols)).astype(jnp.int32)
                picked[live] = (r // per * ncols + col) * per + slot

            live = live + inside * flags[0, r]
            zeros = zeros + (1 - inside) * flags[0, r]
        picked[live] = 0
        zeros = zeros.astype(f32)
        pairs = jnp.minimum((live + 2) // 2, count // 2)
        quads = (2 * pairs + QUAD - 1) // QUAD

        def weight_of(slot):
            return jnp.where(slot < live, 1.0, jnp.where(slot == live, zeros, 0.0))

        def project(j, carry):
            pair = []
            for i in range(2):
                slot = 2 * j + i
                value = x_ref[picked[jnp.minimum(slot, live)]].astype(f32)
                pair.append(jnp.where(slot < live, value, 0.0))
            both = jnp.concatenate(pair, axis=1)
            cells[j] = both
            normed = rms(both, g1).astype(half)
            q_s[j] = rms(dot_t(w_query[...], normed), gq).astype(half)
            k_hat = rms(dot_t(w_key[...], normed), gk).astype(half)
            value = dot_t(w_value[...], normed).astype(half).astype(f32)
            for i in range(2):
                k_s[2 * j + i] = k_hat[:, i * rows : (i + 1) * rows]
                v_s[2 * j + i] = value[:, i * rows : (i + 1) * rows]
            return carry

        lax.fori_loop(0, pairs, project, 0)
        total_s[...] = jnp.zeros_like(total_s)

        def attend(j, carry):
            q_pair = q_s[j]

            def keys_of(k, below):
                keys = k_s[pl.ds(QUAD * k, QUAD)]
                prods = [
                    (keys * q_pair[:, i * rows : (i + 1) * rows][None]).reshape(QUAD * chans, rows)
                    for i in range(2)
                ]
                scores = jnp.dot(
                    spread[...], jnp.concatenate(prods, axis=1), preferred_element_type=f32
                )
                weights = jnp.exp(scores) * weight_of(within + QUAD * k)
                w_s[k] = weights
                return below + weights[:8] + weights[8:]

            below = lax.fori_loop(0, quads, keys_of, jnp.zeros((8, 2 * rows), f32))
            below = below + pltpu.roll(below, HEADS, 0)
            below = jnp.concatenate([below, below], axis=0)

            def values_of(k, above):
                probs = (w_s[k] / below).astype(half)
                wide = jnp.dot(gather[...], probs, preferred_element_type=f32)
                for s in range(QUAD):
                    value = v_s[QUAD * k + s]
                    above = above + wide[s * chans : (s + 1) * chans] * jnp.concatenate(
                        [value, value], axis=1
                    )
                return above

            above = lax.fori_loop(0, quads, values_of, jnp.zeros((chans, 2 * rows), f32))
            mixed = above.astype(half)
            hidden = cells[j] + dot_t(w_out[...], mixed)
            normed = rms(hidden, g2).astype(half)
            inner = jax.nn.gelu(dot_t(w_in[...], normed), approximate=True).astype(half)
            tokens = hidden + jnp.dot(w_back[...], inner, preferred_element_type=f32)
            total_s[...] += tokens[:, :rows] * weight_of(2 * j) + tokens[:, rows:] * weight_of(
                2 * j + 1
            )
            return carry

        lax.fori_loop(0, pairs, attend, 0)
        o_ref[x] = (total_s[...] / flag_sum.astype(f32)).astype(half)
        return carry

    lax.fori_loop(0, cols, column, 0)


MOVES = [(dp, db) for dp in (-1, 0, 1) for db in (-1, 0, 1) if (dp, db) != (0, 0)]


def decode_kernel(sizes, j_ref, w1, w2, o_ref, *scratch):
    nrow, bands, passes = sizes
    bufs = scratch[: len(MOVES)]
    taps, acts, send, recv = scratch[len(MOVES) :]
    cols, chans, rows = j_ref.shape
    p = lax.axis_index("pass")
    b = lax.axis_index("tile") * nrow + lax.axis_index("row")

    def exists(dp, db):
        ok = jnp.bool_(True)
        if dp:
            ok = ok & (p + dp >= 0) & (p + dp < passes)
        if db:
            ok = ok & (b + db >= 0) & (b + db < bands)
        return ok

    def target(dp, db):
        k = b + db
        return {"pass": p + dp, "tile": k // nrow, "row": k % nrow}

    barrier = pltpu.get_barrier_semaphore()
    neighbours = jnp.int32(0)
    for dp, db in MOVES:
        there = exists(dp, db)
        neighbours = neighbours + there.astype(jnp.int32)

        @pl.when(there)
        def _():
            pl.semaphore_signal(barrier, inc=1, device_id=target(dp, db), device_id_type=MESH)

    pl.semaphore_wait(barrier, neighbours)

    def copy_of(n):
        dp, db = MOVES[n]
        src = j_ref
        if dp:
            src = j_ref.at[pl.ds(cols - 2 if dp > 0 else 0, 2)]
        return pltpu.make_async_remote_copy(
            src_ref=src,
            dst_ref=bufs[n],
            send_sem=send.at[n],
            recv_sem=recv.at[n],
            device_id=target(dp, db),
            device_id_type=MESH,
        )

    for n, (dp, db) in enumerate(MOVES):

        @pl.when(exists(dp, db))
        def _():
            copy_of(n).start()

    for n, (dp, db) in enumerate(MOVES):

        @pl.when(exists(-dp, -db))
        def _():
            copy_of(n).wait_recv()

        @pl.when(jnp.logical_not(exists(-dp, -db)))
        def _():
            bufs[n][...] = jnp.zeros_like(bufs[n])

    def side(dp, db):
        return bufs[MOVES.index((-dp, -db))]

    lane = lax.broadcasted_iota(jnp.int32, (chans, rows), 1)
    wide_lane = lax.broadcasted_iota(jnp.int32, (chans, 2 * rows), 1)

    def widen(values):
        last = 2 * rows - 1
        return jnp.concatenate(
            [
                pltpu.roll(values, 1, 1).astype(half),
                values.astype(half),
                pltpu.roll(values, last, 1).astype(half),
            ],
            axis=0,
        )

    for n in range(cols + 4):
        dp = -1 if n < 2 else (1 if n >= cols + 2 else 0)
        at = n if dp < 0 else (n - cols - 2 if dp > 0 else n - 2)
        middle = j_ref[at] if dp == 0 else side(dp, 0)[at]
        border = jnp.where(
            lane < rows // 2, side(dp, 1)[at].astype(f32), side(dp, -1)[at].astype(f32)
        )
        taps[n] = widen(jnp.concatenate([middle.astype(f32), border], axis=1))
    row_pos = b * rows + jnp.where(wide_lane < rows + rows // 2, wide_lane, wide_lane - 2 * rows)
    row_inside = (row_pos >= 0) & (row_pos < bands * rows)
    for n in range(cols + 2):
        near = taps[n : n + 3].reshape(9 * chans, 2 * rows)
        act = jax.nn.gelu(dot_t(w1[...], near), approximate=True)
        col_pos = p * cols + n - 1
        inside = row_inside & (col_pos >= 0) & (col_pos < passes * cols)
        acts[n] = widen(jnp.where(inside, act, 0.0))
    for n in range(cols):
        near = acts[n : n + 3, :, :rows].reshape(9 * chans, rows)
        o_ref[:, n, :] = dot_t(w2[...], near)

    for n, (dp, db) in enumerate(MOVES):

        @pl.when(exists(dp, db))
        def _():
            copy_of(n).wait_send()


def local(
    groups,
    nrow,
    bands,
    passes,
    revisits,
    shifts,
    flags,
    norm1_gain,
    w_query,
    w_key,
    w_value,
    query_gain,
    key_gain,
    w_out,
    norm2_gain,
    w_in,
    w_back,
    conv_first,
    conv_second,
):
    sizes = (nrow, bands, passes)
    per, own_cols, chans, all_rows = revisits.shape
    rows = all_rows // bands
    ncols = own_cols * bands
    cols = ncols // passes
    count = per * passes
    side_effects = dict(has_side_effects=True, vmem_limit_bytes=GRANT)
    dma = pltpu.SemaphoreType.DMA
    total = groups * passes
    metas, level = pl.pallas_call(
        functools.partial(census_kernel, (groups, passes), ncols),
        out_shape=(
            jax.ShapeDtypeStruct((passes, 2, per), jnp.int32),
            jax.ShapeDtypeStruct((1,), jnp.int32),
        ),
        in_specs=[whole()],
        out_specs=(whole(), whole(pltpu.SMEM)),
        scratch_shapes=[
            pltpu.VMEM((total, 2, per), jnp.int32),
            dma((max(total - 1, 1),)),
            dma((max(total - 1, 1),)),
        ],
        compiler_params=pltpu.CompilerParams(collective_id=0, **side_effects),
        name="census",
    )(shifts.T)
    shifted = pl.pallas_call(
        functools.partial(shift_kernel, (nrow, ncols)),
        out_shape=jax.ShapeDtypeStruct((bands, own_cols, per, chans, rows), half),
        in_specs=[whole(pltpu.SMEM), whole()],
        out_specs=whole(),
        compiler_params=pltpu.CompilerParams(vmem_limit_bytes=GRANT),
        name="row_shift",
    )(shifts.T, revisits)
    others = max(passes - 1, 1)

    def exchange(index):
        return pl.pallas_call(
            functools.partial(gather_kernel, sizes, index + 1),
            out_shape=jax.ShapeDtypeStruct((passes, bands, own_cols, per, chans, rows), half),
            in_specs=[whole()],
            out_specs=whole(pl.ANY),
            scratch_shapes=[
                dma((1,)),
                dma((bands,)),
                dma((bands,)),
                dma((others, bands)),
                dma((others, bands)),
            ],
            compiler_params=pltpu.CompilerParams(collective_id=2 + index, **side_effects),
            name="exchange",
        )

    banded = lax.switch(level[0] - 1, [exchange(i) for i in range(per)], shifted)
    banded = banded.reshape(passes * ncols * per, chans, rows)
    gains = jnp.broadcast_to(
        jnp.stack([norm1_gain, query_gain, key_gain, norm2_gain])[:, :, None], (4, chans, rows)
    )
    head_size = chans // HEADS
    slots, heads = np.divmod(np.arange(QUAD * HEADS), HEADS)
    at = np.arange(QUAD * chans)
    match = (slots[:, None] == at[None] // chans) & (heads[:, None] == at[None] % chans // head_size)
    spread = jnp.asarray(match * (1.0 / math.sqrt(head_size)), half)
    gather = jnp.asarray(match.T, half)
    joined = pl.pallas_call(
        functools.partial(join_kernel, cols, ncols),
        out_shape=jax.ShapeDtypeStruct((cols, chans, rows), half),
        in_specs=[whole(pltpu.SMEM), whole(pltpu.SMEM)] + [whole()] * 10,
        out_specs=whole(),
        scratch_shapes=[
            pltpu.VMEM((count // 2, chans, 2 * rows), f32),
            pltpu.VMEM((count // 2, chans, 2 * rows), half),
            pltpu.VMEM((count, chans, rows), half),
            pltpu.VMEM((count, chans, rows), f32),
            pltpu.VMEM((count // QUAD, QUAD * HEADS, 2 * rows), f32),
            pltpu.VMEM((chans, rows), f32),
            pltpu.SMEM((count + 1,), jnp.int32),
        ],
        compiler_params=pltpu.CompilerParams(vmem_limit_bytes=GRANT),
        name="join",
    )(metas, flags.T, banded, gains, spread, gather, w_query, w_key, w_value, w_out, w_in, w_back.T)
    outs = conv_second.shape[3]
    decoded = pl.pallas_call(
        functools.partial(decode_kernel, sizes),
        out_shape=jax.ShapeDtypeStruct((outs, cols, rows), f32),
        in_specs=[whole()] * 3,
        out_specs=whole(),
        scratch_shapes=[
            pltpu.VMEM((2 if dp else cols, chans, rows), half) for dp, db in MOVES
        ]
        + [
            pltpu.VMEM((cols + 4, 3 * chans, 2 * rows), half),
            pltpu.VMEM((cols + 2, 3 * chans, 2 * rows), half),
            dma((len(MOVES),)),
            dma((len(MOVES),)),
        ],
        compiler_params=pltpu.CompilerParams(collective_id=1, **side_effects),
        name="decode",
    )(joined, conv_first.reshape(9 * chans, -1), conv_second.reshape(9 * chans, outs))
    return jnp.transpose(decoded, (1, 0, 2))


def solution(mesh):
    shape = mesh.shape
    fixed = [P()] * 12
    return jax.shard_map(
        functools.partial(local, shape["groups"], shape["row"], shape["tile"] * shape["row"], shape["pass"]),
        mesh=mesh,
        in_specs=(
            P(("groups", "pass"), ("tile", "row"), None, None),
            P(("groups", "pass"), None),
            P("groups", ("tile", "row")),
            *fixed,
        ),
        out_specs=P(("groups", "pass"), None, ("tile", "row")),
        check_vma=False,
    )
```
